32 devices in a mesh: gz: 2 (over y), row: 4 (over x, core), col: 4 (over z).
Axes of the slice: x: 2, y: 2, z: 4, core: 2. Of those that a mesh axis runs over, the one named last changes fastest.
Arguments:
- anc_lower: bfloat16 [1, 1024, 1024], P(None, 'col', 'row'), may hold values from -0.125 to 0.125
- anc_upper: bfloat16 [1, 1024, 1024], P(None, 'col', 'row'), may hold values from -0.125 to 0.125
- sub_lower: bfloat16 [16, 1024, 1024], P('gz', 'col', 'row'), may hold values from -0.125 to 0.125
- sub_upper: bfloat16 [16, 1024, 1024], P('gz', 'col', 'row'), may hold values from -0.125 to 0.125
- anc_rhs: bfloat16 [1, 1024, 64], P(None, 'col'), may hold values from -6 to 6
- sub_rhs: bfloat16 [6, 1024, 64], P('gz', 'col'), may hold values from -6 to 6
- layer_subtree: int32 [2], replicated, may hold values from 0 to 1, each once
- sub_pattern: int32 [10, 2], P('gz'), may hold values 0 or 1
Outputs:
- anc_solution: float32 [1, 1024, 64], P(None, ('row', 'col'))
- sub_solution: float32 [6, 1024, 64], P('gz', ('row', 'col'))
The draws below stay inside these ranges and needn't reach their ends.
Inputs may be any that keep to these rules, and one draw needn't show every extreme that they name: `layer_subtree`: each subtree is held by exactly one layer.
All inputs are finite; a program needn't handle non-finite values. No bound on the sum of `sub_pattern` on one device may be relied on, other than what follows from the above.
Results may differ from the reference program's by a relative error of at most 0.018.
Values may be sent and summed in bfloat16 or wider, within the bound.
A program may use at most 64 MiB of HBM per device.

```python
import jax
import jax.numpy as jnp
import numpy as np

S = 1024
R = 64
SUB_LEVELS = 2
SUB_NODES = 3
ANC_NODES = 1
SUB_PAIRS = 5
ANC_PAIRS = 0
N_GZ = 2


def place_ends(result, stream_key, low, high):
    longest = result.shape.index(max(result.shape))
    spots = []
    for shift in (0, 1):
        where = [jax.random.randint(jax.random.fold_in(stream_key, axis), (), 0, length) for axis, length in enumerate(result.shape)]
        where[longest] = (where[longest] + shift) % result.shape[longest]
        spots.append(tuple(where))
    return result.at[spots[0]].set(low).at[spots[1]].set(high)


def level_of(key, shape, pieces, low, top_value):
    def one(dim, parts):
        steps = jax.random.uniform(jax.random.fold_in(jax.random.fold_in(key, 6), dim), (parts,), jnp.float32, low / len(pieces), top_value / len(pieces))
        return jnp.repeat(jnp.exp(steps), shape[dim] // parts).reshape((-1,) + (1,) * (len(shape) - dim - 1))

    loudness = one(*pieces[0])
    for cut in pieces[1:]:
        loudness = loudness * one(*cut)
    return loudness


def noise(key, dims, spread, reach, pieces=(), kind=jnp.bfloat16):
    result = spread * jax.random.normal(key, dims, jnp.float32)
    if pieces:
        result = result * level_of(key, dims, pieces, -0.22, 0.18)
    return jnp.clip(result, -reach, reach).astype(kind)


def setup_inputs(seed: int = 0) -> dict:
    key_of = jax.random.split(jax.random.key(seed), 9)
    return {
        "anc_lower": noise(key_of[0], (ANC_NODES + ANC_PAIRS, S, S), (2 * S) ** -0.5, 0.125, ((1, 4), (2, 4))),
        "anc_upper": noise(key_of[1], (ANC_NODES + ANC_PAIRS, S, S), (2 * S) ** -0.5, 0.125, ((1, 4), (2, 4))),
        "sub_lower": noise(key_of[2], (N_GZ * (SUB_NODES + SUB_PAIRS), S, S), (2 * S) ** -0.5, 0.125, ((0, 2), (1, 4), (2, 4))),
        "sub_upper": noise(key_of[3], (N_GZ * (SUB_NODES + SUB_PAIRS), S, S), (2 * S) ** -0.5, 0.125, ((0, 2), (1, 4), (2, 4))),
        "anc_rhs": noise(key_of[4], (ANC_NODES, S, R), 1.0, 6.0, ((1, 4),)),
        "sub_rhs": noise(key_of[5], (N_GZ * SUB_NODES, S, R), 1.0, 6.0, ((0, 2), (1, 4))),
        "layer_subtree": jax.random.permutation(key_of[6], N_GZ).astype(jnp.int32),
        "sub_pattern": place_ends((jax.random.randint(key_of[7], (N_GZ * SUB_PAIRS, 2), 0, 4) < 3).astype(jnp.int32), jax.random.fold_in(key_of[7], 1), 0, 1),
    }


def subtree_pairs(levels):
    listed = []
    for member in range(SUB_NODES):
        height = (member + 1).bit_length() - 1
        for global_level in range(levels):
            listed.append((member, 0, global_level))
        for local_level in range(height):
            listed.append((member, 1, ((member + 1) >> (height - local_level)) - 1))
    return listed


def ancestor_pairs(levels):
    listed = []
    for member in range(2 ** levels - 1):
        height = (member + 1).bit_length() - 1
        for upper_level in range(height):
            listed.append((member, ((member + 1) >> (height - upper_level)) - 1))
    return listed


def level_span(depth_now):
    return 2 ** depth_now - 1, 2 ** (depth_now + 1) - 1


def apply_pair(matrix, vectors):
    return jnp.einsum("...ik,...kr->...ir", matrix.astype(jnp.float32), vectors.astype(jnp.float32))


def apply_inverse(matrix, vectors):
    return jnp.einsum("...ki,...kr->...ir", matrix.astype(jnp.float32), vectors.astype(jnp.float32))


def reference(anc_lower, anc_upper, sub_lower, sub_upper, anc_rhs, sub_rhs, layer_subtree, sub_pattern):
    layers = N_GZ
    levels = layers.bit_length() - 1
    anc_count = layers - 1
    sub_list = subtree_pairs(levels)
    anc_list = ancestor_pairs(levels)
    pair_count = len(sub_list)
    low_blocks = sub_lower.reshape(layers, SUB_NODES + pair_count, S, S)
    up_blocks = sub_upper.reshape(layers, SUB_NODES + pair_count, S, S)
    given_sub = sub_rhs.reshape(layers, SUB_NODES, S, R)
    pattern = sub_pattern.reshape(layers, pair_count, 2).astype(jnp.float32)
    powers = jnp.asarray(2 ** (levels - np.arange(levels)), jnp.int32)
    heap_ids = (layer_subtree[:, None] + layers) // powers[None, :] - 1
    choose = (heap_ids[:, :, None] == jnp.arange(anc_count, dtype=jnp.int32)[None, None, :]).astype(jnp.float32)

    sub_acc = [jnp.zeros((layers, S, R), jnp.float32) for member in range(SUB_NODES)]
    to_anc = jnp.zeros((anc_count, S, R), jnp.float32)
    sub_rows = [None] * SUB_NODES
    for depth_now in reversed(range(SUB_LEVELS)):
        first_id, stop_id = level_span(depth_now)
        for member in range(first_id, stop_id):
            residual = (given_sub[:, member].astype(jnp.float32) - sub_acc[member]).astype(jnp.bfloat16)
            sub_rows[member] = apply_inverse(low_blocks[:, member], residual).astype(jnp.bfloat16)
        for position, (source, pair_kind, target) in enumerate(sub_list):
            if first_id <= source < stop_id:
                update = apply_pair(low_blocks[:, SUB_NODES + position], sub_rows[source])
                update = update * pattern[:, position, 0][:, None, None]
                if pair_kind == 1:
                    sub_acc[target] = sub_acc[target] + update
                else:
                    to_anc = to_anc + jnp.einsum("ga,gir->air", choose[:, target], update)

    anc_acc = [jnp.zeros((S, R), jnp.float32) for member in range(anc_count)]
    anc_rows = [None] * anc_count
    for depth_now in reversed(range(levels)):
        first_id, stop_id = level_span(depth_now)
        for member in range(first_id, stop_id):
            residual = (anc_rhs[member].astype(jnp.float32) - to_anc[member] - anc_acc[member]).astype(jnp.bfloat16)
            anc_rows[member] = apply_inverse(anc_lower[member], residual).astype(jnp.bfloat16)
        for position, (source, target) in enumerate(anc_list):
            if first_id <= source < stop_id:
                anc_acc[target] = anc_acc[target] + apply_pair(anc_lower[anc_count + position], anc_rows[source])

    anc_z = [None] * anc_count
    anc_out = [None] * anc_count
    for depth_now in range(levels):
        first_id, stop_id = level_span(depth_now)
        for member in range(first_id, stop_id):
            running = anc_rows[member].astype(jnp.float32)
            for position, (source, target) in enumerate(anc_list):
                if source == member:
                    running = running - apply_pair(anc_upper[anc_count + position], anc_z[target])
            solved = apply_inverse(anc_upper[member], running.astype(jnp.bfloat16))
            anc_out[member] = solved
            anc_z[member] = solved.astype(jnp.bfloat16)

    selected = jnp.einsum("gea,air->geir", choose, jnp.stack(anc_z).astype(jnp.float32)).astype(jnp.bfloat16)
    sub_z = [None] * SUB_NODES
    sub_out = [None] * SUB_NODES
    for depth_now in range(SUB_LEVELS):
        first_id, stop_id = level_span(depth_now)
        for member in range(first_id, stop_id):
            running = sub_rows[member].astype(jnp.float32)
            for position, (source, pair_kind, target) in enumerate(sub_list):
                if source == member:
                    anchor = selected[:, target] if pair_kind == 0 else sub_z[target]
                    update = apply_pair(up_blocks[:, SUB_NODES + position], anchor)
                    running = running - update * pattern[:, position, 1][:, None, None]
            solved = apply_inverse(up_blocks[:, member], running.astype(jnp.bfloat16))
            sub_out[member] = solved
            sub_z[member] = solved.astype(jnp.bfloat16)
    return jnp.stack(anc_out), jnp.stack(sub_out, 1).reshape(layers * SUB_NODES, S, R)
```

```python
import functools

import jax
import jax.numpy as jnp
import numpy as np
from jax import lax
from jax.experimental import pallas as pl
from jax.experimental.pallas import tpu as pltpu
from jax.sharding import PartitionSpec as P

R = 64
SUB_LEVELS = 2
SUB_NODES = 3


def level_span(depth_now):
    return (2**depth_now - 1, 2 ** (depth_now + 1) - 1)


def local_routes(first_id, stop_id, depth_now, target_count):
    table = np.zeros((target_count, (stop_id - first_id) * depth_now), np.float32)
    for offset, member in enumerate(range(first_id, stop_id)):
        for local_level in range(depth_now):
            target = (member + 1 >> depth_now - local_level) - 1
            table[target, offset * depth_now + local_level] = 1.0
    return table


def solve_diagonal(residual, blocks):
    whole_blocks = lax.all_gather(blocks, "col", axis=1, tiled=True)
    whole_res = lax.all_gather(residual, "col", axis=1, tiled=True)
    rows_full = jnp.einsum(
        "nki,nkr->nir", whole_blocks, whole_res, preferred_element_type=jnp.float32
    )
    share = rows_full.shape[1] // lax.axis_size("col")
    owned = lax.dynamic_slice_in_dim(rows_full, lax.axis_index("col") * share, share, 1)
    return (owned, rows_full.astype(jnp.bfloat16))


def upper_sum(values):
    return lax.psum(values, "row")


def local(anc_lower, anc_upper, sub_lower, sub_upper, anc_rhs, sub_rhs, layer_subtree, sub_pattern):
    layers = lax.axis_size("gz")
    levels = layers.bit_length() - 1
    anc_count = layers - 1
    row_count = lax.axis_size("row")
    col_count = lax.axis_size("col")
    rows_here = anc_lower.shape[2]
    cols_here = anc_lower.shape[1]
    sub_start = [0]
    for member in range(SUB_NODES):
        sub_start.append(sub_start[-1] + levels + (member + 1).bit_length() - 1)
    anc_start = [0]
    for member in range(anc_count):
        anc_start.append(anc_start[-1] + (member + 1).bit_length() - 1)
    low_pattern = sub_pattern[:, 0].astype(jnp.float32)
    up_pattern = sub_pattern[:, 1].astype(jnp.float32)
    layer_here = lax.axis_index("gz")
    subtree = jnp.sum(
        jnp.where(jnp.arange(layers, dtype=jnp.int32) == layer_here, layer_subtree, 0)
    )
    powers = jnp.asarray(2 ** (levels - np.arange(levels)), jnp.int32)
    heap_ids = (subtree + layers) // powers - 1
    choose = (heap_ids[:, None] == jnp.arange(anc_count, dtype=jnp.int32)[None, :]).astype(
        jnp.float32
    )
    first_layer = (layer_here == 0).astype(jnp.float32)
    row_index = lax.axis_index("row")
    col_index = lax.axis_index("col")
    holds_piece = (row_index == col_index * row_count // col_count).astype(jnp.float32)
    piece_start = jnp.clip(col_index * cols_here - row_index * rows_here, 0, rows_here - cols_here)

    def own_piece(rows_block):
        return holds_piece * lax.dynamic_slice_in_dim(rows_block, piece_start, cols_here, 1).astype(
            jnp.float32
        )

    sub_acc = jnp.zeros((SUB_NODES, cols_here, R), jnp.float32)
    to_anc = jnp.zeros((anc_count, cols_here, R), jnp.float32)
    sub_rows = {}
    for depth_now in reversed(range(SUB_LEVELS)):
        first_id, stop_id = level_span(depth_now)
        node_count = stop_id - first_id
        given = sub_rhs[first_id:stop_id].astype(jnp.float32)
        if depth_now + 1 < SUB_LEVELS:
            given = given - lax.psum(sub_acc[first_id:stop_id], "row")
        unused, solved = solve_diagonal(given.astype(jnp.bfloat16), sub_lower[first_id:stop_id])
        sub_rows[depth_now] = solved
        per_node = levels + depth_now
        opening = SUB_NODES + sub_start[first_id]
        blocks = sub_lower[opening : opening + node_count * per_node].reshape(
            node_count, per_node, cols_here, rows_here
        )
        weights = low_pattern[sub_start[first_id] : sub_start[stop_id]].reshape(
            node_count, per_node
        )
        updates = jnp.einsum("npik,nkr->npir", blocks, solved, preferred_element_type=jnp.float32)
        updates = updates * weights[:, :, None, None]
        to_anc = to_anc + jnp.einsum("ea,eir->air", choose, jnp.sum(updates[:, :levels], 0))
        if depth_now > 0:
            table = jnp.asarray(local_routes(first_id, stop_id, depth_now, SUB_NODES))
            sub_acc = sub_acc + jnp.einsum(
                "tq,qir->tir", table, updates[:, levels:].reshape(-1, cols_here, R)
            )
    anc_acc = jnp.zeros((anc_count, cols_here, R), jnp.float32)
    anc_rows = {}
    for depth_now in reversed(range(levels)):
        first_id, stop_id = level_span(depth_now)
        node_count = stop_id - first_id
        joined = to_anc[first_id:stop_id] + first_layer * anc_acc[first_id:stop_id]
        reached = lax.psum(joined, ("gz", "row"))
        given = anc_rhs[first_id:stop_id].astype(jnp.float32) - reached
        unused, solved = solve_diagonal(given.astype(jnp.bfloat16), anc_lower[first_id:stop_id])
        anc_rows[depth_now] = solved
        if depth_now > 0:
            opening = anc_count + anc_start[first_id]
            blocks = anc_lower[opening : opening + node_count * depth_now].reshape(
                node_count, depth_now, cols_here, rows_here
            )
            updates = jnp.einsum(
                "npik,nkr->npir", blocks, solved, preferred_element_type=jnp.float32
            )
            table = jnp.asarray(local_routes(first_id, stop_id, depth_now, anc_count))
            anc_acc = anc_acc + jnp.einsum("tq,qir->tir", table, updates.reshape(-1, cols_here, R))
    anc_z_parts = []
    anc_out_parts = []
    for depth_now in range(levels):
        first_id, stop_id = level_span(depth_now)
        node_count = stop_id - first_id
        given = own_piece(anc_rows[depth_now])
        if depth_now > 0:
            z_sofar = jnp.concatenate(anc_z_parts, 0)
            table = local_routes(first_id, stop_id, depth_now, anc_count)[:first_id].T
            sources = jnp.einsum(
                "qa,akr->qkr",
                jnp.asarray(table, jnp.bfloat16),
                z_sofar,
                preferred_element_type=jnp.float32,
            )
            sources = sources.astype(jnp.bfloat16).reshape(node_count, depth_now, rows_here, R)
            opening = anc_count + anc_start[first_id]
            blocks = anc_upper[opening : opening + node_count * depth_now].reshape(
                node_count, depth_now, cols_here, rows_here
            )
            updates = jnp.einsum(
                "npik,npkr->npir", blocks, sources, preferred_element_type=jnp.float32
            )
            given = given - jnp.sum(updates, 1)
        summed = upper_sum(given)
        owned, solved = solve_diagonal(summed.astype(jnp.bfloat16), anc_upper[first_id:stop_id])
        anc_out_parts.append(owned)
        anc_z_parts.append(solved)
    anc_z_all = jnp.concatenate(anc_z_parts, 0)
    selected = jnp.einsum(
        "ea,akr->ekr", choose.astype(jnp.bfloat16), anc_z_all, preferred_element_type=jnp.float32
    )
    selected = selected.astype(jnp.bfloat16)
    sub_z_parts = []
    sub_out_parts = []
    for depth_now in range(SUB_LEVELS):
        first_id, stop_id = level_span(depth_now)
        node_count = stop_id - first_id
        per_node = levels + depth_now
        opening = SUB_NODES + sub_start[first_id]
        blocks = sub_upper[opening : opening + node_count * per_node].reshape(
            node_count, per_node, cols_here, rows_here
        )
        weights = up_pattern[sub_start[first_id] : sub_start[stop_id]].reshape(node_count, per_node)
        updates = jnp.einsum(
            "npik,pkr->npir", blocks[:, :levels], selected, preferred_element_type=jnp.float32
        )
        if depth_now > 0:
            z_sofar = sub_z_parts[0]
            table = local_routes(first_id, stop_id, depth_now, SUB_NODES)[:first_id].T
            sources = jnp.einsum(
                "qa,akr->qkr",
                jnp.asarray(table, jnp.bfloat16),
                z_sofar,
                preferred_element_type=jnp.float32,
            )
            sources = sources.astype(jnp.bfloat16).reshape(node_count, depth_now, rows_here, R)
            local_updates = jnp.einsum(
                "npik,npkr->npir", blocks[:, levels:], sources, preferred_element_type=jnp.float32
            )
            updates = jnp.concatenate([updates, local_updates], 1)
        change = jnp.sum(updates * weights[:, :, None, None], 1)
        summed = upper_sum(own_piece(sub_rows[depth_now]) - change)
        owned, solved = solve_diagonal(summed.astype(jnp.bfloat16), sub_upper[first_id:stop_id])
        sub_out_parts.append(owned)
        sub_z_parts.append(solved)
    return (jnp.concatenate(anc_out_parts, 0), jnp.concatenate(sub_out_parts, 0))


BF = jnp.bfloat16
F32 = jnp.float32
MESH = pl.DeviceIdType.MESH


def times(vectors, block):
    return jnp.dot(vectors, block, preferred_element_type=F32)


def times_t(vectors, block):
    return lax.dot_general(vectors, block, (((1,), (1,)), ((), ())), preferred_element_type=F32)


def flip(rows):
    return jnp.transpose(rows.astype(F32))


def fused_kernel(
    layers,
    rows_n,
    cols_n,
    anc_lower,
    anc_upper,
    sub_lower,
    sub_upper,
    anc_rhs,
    sub_rhs,
    layer_subtree,
    pattern,
    anc_out,
    sub_out,
    al,
    au,
    sl,
    su,
    ar,
    sr,
    pair_send,
    pair_recv,
    one_send,
    one_recv,
    all_send,
    all_recv,
    diag_recv,
    flipped,
    piece_send,
    piece_recv,
    load_sem,
    send_sem,
    recv_sem,
):
    gz = lax.axis_index("gz")
    row = lax.axis_index("row")
    col = lax.axis_index("col")
    loads = {}

    def load(name, source, target):
        copy = pltpu.make_async_copy(source, target, load_sem.at[len(loads)])
        copy.start()
        loads[name] = copy

    load("sr", sub_rhs, sr)
    load("e12", sub_lower.at[pl.ds(1, 2)], sl.at[pl.ds(1, 2)])
    load("low", sub_lower.at[pl.ds(3, 5)], sl.at[pl.ds(3, 5)])
    load("e0", sub_lower.at[0], sl.at[0])
    load("ar", anc_rhs, ar)
    load("al", anc_lower, al)
    load("au", anc_upper, au)
    load("su", sub_upper, su)

    def row_peer(j):
        return (gz, lax.rem(row + j, rows_n), col)

    def col_peer(j):
        return (gz, row, lax.rem(col + j, cols_n))

    barrier = pltpu.get_barrier_semaphore()
    peers = [row_peer(j) for j in range(1, rows_n)] + [col_peer(j) for j in range(1, cols_n)]
    wide = [
        (lax.rem(gz + g, layers), lax.rem(row + j, rows_n), col)
        for g in range(layers)
        for j in range(rows_n)
        if g or j
    ]
    peers = peers + wide[rows_n - 1 :]
    for peer in peers:
        pl.semaphore_signal(barrier, inc=1, device_id=peer, device_id_type=MESH)

    started = []

    def send(step, source, target, peer_list):
        made = []
        for j, peer in enumerate(peer_list):
            copy = pltpu.make_async_remote_copy(
                src_ref=source(j),
                dst_ref=target(j),
                send_sem=send_sem.at[step, j],
                recv_sem=recv_sem.at[step, j],
                device_id=peer,
                device_id_type=MESH,
            )
            copy.start()
            made.append(copy)
        started.extend(made)
        return made

    def swap(step, values, peer_list, send_buf, recv_buf, between=None):
        for n, value in enumerate(values):
            send_buf[n] = value.astype(BF)
        made = send(step, lambda j: send_buf, lambda j: recv_buf.at[j], peer_list)
        extra = between() if between is not None else None
        sums = list(values)
        for j, copy in enumerate(made):
            copy.wait_recv()
            for n in range(len(sums)):
                sums[n] = sums[n] + recv_buf[j, n].astype(F32)
        return sums, extra

    row_list = [row_peer(j) for j in range(1, rows_n)]
    col_list = [col_peer(j) for j in range(1, cols_n)]

    anc_here = jnp.where((layers + layer_subtree[gz]) // layers - 1 == 0, 1, 0)
    low = [pattern[p, 0] for p in range(5)]
    up = [pattern[p, 1] for p in range(5)]
    low = [(w * anc_here if p in (0, 1, 3) else w).astype(F32) for p, w in enumerate(low)]
    up = [(w * anc_here if p in (0, 1, 3) else w).astype(F32) for p, w in enumerate(up)]
    on_diag = jnp.where(row == col, 1.0, 0.0).astype(F32)

    loads["sr"].wait()
    r1 = flip(sr[1]).astype(BF)
    r2 = flip(sr[2]).astype(BF)
    loads["e12"].wait()
    part1 = times(r1, sl[1])
    part2 = times(r2, sl[2])
    pl.semaphore_wait(barrier, len(peers))

    def between_a():
        loads["ar"].wait()
        return flip(sr[0]), flip(ar[0])

    (y1, y2), (given0, given_anc) = swap(
        0, [part1, part2], col_list, pair_send.at[0], pair_recv.at[0], between_a
    )
    y1 = y1.astype(BF)
    y2 = y2.astype(BF)
    loads["low"].wait()
    change = low[2] * times_t(y1, sl[5]) + low[4] * times_t(y2, sl[7])

    def between_b():
        loads["e0"].wait()
        return low[1] * times_t(y1, sl[4]) + low[3] * times_t(y2, sl[6])

    (change,), to_anc = swap(1, [change], row_list, one_send.at[0], one_recv.at[0], between_b)
    r0 = (given0 - change).astype(BF)
    (y0,), unused = swap(2, [times(r0, sl[0])], col_list, one_send.at[1], one_recv.at[1])
    y0 = y0.astype(BF)

    to_anc = to_anc + low[0] * times_t(y0, sl[3])
    (reached,), unused = swap(3, [to_anc], wide, all_send, all_recv)
    ra = (given_anc - reached).astype(BF)
    loads["al"].wait()
    part = times(ra, al[0])

    one_send[2, 0] = part.astype(BF)

    @pl.when(row != col)
    def to_diag():
        slot = lax.rem(col - row + cols_n - 1, cols_n)
        copy = pltpu.make_async_remote_copy(
            src_ref=one_send.at[2],
            dst_ref=one_recv.at[2, slot],
            send_sem=send_sem.at[4, 0],
            recv_sem=recv_sem.at[4, slot],
            device_id=(gz, row, row),
            device_id_type=MESH,
        )
        copy.start()
        copy.wait_send()

    spread = [
        pltpu.make_async_remote_copy(
            src_ref=one_send.at[3],
            dst_ref=diag_recv,
            send_sem=send_sem.at[5, j],
            recv_sem=recv_sem.at[5, 0],
            device_id=peer,
            device_id_type=MESH,
        )
        for j, peer in enumerate(row_list)
    ]

    @pl.when(row == col)
    def at_diag():
        total = part
        for j in range(cols_n - 1):
            pltpu.make_async_remote_copy(
                src_ref=one_send.at[2],
                dst_ref=one_recv.at[2, j],
                send_sem=send_sem.at[4, 0],
                recv_sem=recv_sem.at[4, j],
                device_id=(gz, row, col),
                device_id_type=MESH,
            ).wait_recv()
            total = total + one_recv[2, j, 0].astype(F32)
        one_send[3, 0] = total.astype(BF)
        for copy in spread:
            copy.start()
        diag_recv[0] = total.astype(BF)
        for copy in spread:
            copy.wait_send()

    @pl.when(row != col)
    def off_diag():
        spread[0].wait_recv()

    ta = diag_recv[0]

    loads["au"].wait()
    loads["su"].wait()
    (za_full,), unused = swap(6, [times(ta, au[0])], col_list, one_send.at[4], one_recv.at[4])
    za = za_full.astype(BF)
    piece = za_full.shape[1] // cols_n
    mine = pl.ds(pl.multiple_of(col * piece, piece), piece)

    part = on_diag * y0.astype(F32) - up[0] * times_t(za, su[3])

    def between_i():
        flipped[0] = jnp.transpose(za_full)
        anc_out[0] = flipped[0, mine, :]
        return (
            on_diag * y1.astype(F32) - up[1] * times_t(za, su[4]),
            on_diag * y2.astype(F32) - up[3] * times_t(za, su[6]),
        )

    (t0,), (s1, s2) = swap(7, [part], row_list, one_send.at[5], one_recv.at[5], between_i)
    (z0_full,), unused = swap(
        8, [times(t0.astype(BF), su[0])], col_list, one_send.at[6], one_recv.at[6]
    )
    z0 = z0_full.astype(BF)

    s1 = s1 - up[2] * times_t(z0, su[5])
    s2 = s2 - up[4] * times_t(z0, su[7])

    def between_k():
        flipped[1] = jnp.transpose(z0_full)
        sub_out[0] = flipped[1, mine, :]

    (t1, t2), unused = swap(9, [s1, s2], row_list, pair_send.at[1], pair_recv.at[1], between_k)
    part1 = times(t1.astype(BF), su[1])
    part2 = times(t2.astype(BF), su[2])
    for c in range(cols_n):
        lanes = slice(c * piece, (c + 1) * piece)
        piece_send[c] = jnp.concatenate([part1[:, lanes], part2[:, lanes]], 1).astype(BF)
    made = send(
        10,
        lambda j: piece_send.at[lax.rem(col + j + 1, cols_n)],
        lambda j: piece_recv.at[j],
        col_list,
    )
    total = piece_send[col].astype(F32)
    for j, copy in enumerate(made):
        copy.wait_recv()
        total = total + piece_recv[j].astype(F32)
    total = jnp.transpose(total)
    sub_out[1] = total[:piece]
    sub_out[2] = total[piece:]
    for copy in started:
        copy.wait_send()


def fused(mesh):
    layers, rows_n, cols_n = (mesh.shape[a] for a in ("gz", "row", "col"))

    def local_fused(*args):
        anc_lower, anc_upper, sub_lower, sub_upper, anc_rhs, sub_rhs, subtree, pattern = args
        cut, right = anc_rhs.shape[1], anc_rhs.shape[2]
        piece = cut // cols_n
        vec = (right, cut)
        peers_n = max(rows_n, cols_n) - 1
        hbm = pl.BlockSpec(memory_space=pl.ANY)
        smem = pl.BlockSpec(memory_space=pltpu.SMEM)
        vmem = pl.BlockSpec(memory_space=pltpu.VMEM)
        return pl.pallas_call(
            functools.partial(fused_kernel, layers, rows_n, cols_n),
            out_shape=(
                jax.ShapeDtypeStruct((1, piece, right), F32),
                jax.ShapeDtypeStruct((SUB_NODES, piece, right), F32),
            ),
            in_specs=[hbm] * 6 + [smem] * 2,
            out_specs=(vmem, vmem),
            scratch_shapes=[
                pltpu.VMEM(anc_lower.shape, BF),
                pltpu.VMEM(anc_upper.shape, BF),
                pltpu.VMEM(sub_lower.shape, BF),
                pltpu.VMEM(sub_upper.shape, BF),
                pltpu.VMEM(anc_rhs.shape, BF),
                pltpu.VMEM(sub_rhs.shape, BF),
                pltpu.VMEM((2, 2) + vec, BF),
                pltpu.VMEM((2, peers_n, 2) + vec, BF),
                pltpu.VMEM((7, 1) + vec, BF),
                pltpu.VMEM((7, peers_n, 1) + vec, BF),
                pltpu.VMEM((1,) + vec, BF),
                pltpu.VMEM((layers * rows_n - 1, 1) + vec, BF),
                pltpu.VMEM((1,) + vec, BF),
                pltpu.VMEM((2, cut, right), F32),
                pltpu.VMEM((cols_n, right, 2 * piece), BF),
                pltpu.VMEM((cols_n - 1, right, 2 * piece), BF),
                pltpu.SemaphoreType.DMA((8,)),
                pltpu.SemaphoreType.DMA((11, layers * rows_n)),
                pltpu.SemaphoreType.DMA((11, layers * rows_n)),
            ],
            compiler_params=pltpu.CompilerParams(collective_id=0, has_side_effects=True),
        )(*args)

    return local_fused


def solution(mesh):
    in_specs = (
        P(None, "col", "row"),
        P(None, "col", "row"),
        P("gz", "col", "row"),
        P("gz", "col", "row"),
        P(None, "col", None),
        P("gz", "col", None),
        P(),
        P("gz", None),
    )
    out_specs = (P(None, ("row", "col"), None), P("gz", ("row", "col"), None))
    one_anc = mesh.shape["gz"] == 2
    square = mesh.shape["row"] == mesh.shape["col"] == 4
    body = fused(mesh) if one_anc and square else local
    return jax.shard_map(body, mesh=mesh, in_specs=in_specs, out_specs=out_specs, check_vma=False)
```

```python
import functools

import jax
import jax.numpy as jnp
import numpy as np
from jax import lax
from jax.experimental import pallas as pl
from jax.experimental.pallas import tpu as pltpu
from jax.sharding import PartitionSpec as P

R = 64
SUB_LEVELS = 2
SUB_NODES = 3


def level_span(depth_now):
    return (2**depth_now - 1, 2 ** (depth_now + 1) - 1)


def local_routes(first_id, stop_id, depth_now, target_count):
    table = np.zeros((target_count, (stop_id - first_id) * depth_now), np.float32)
    for offset, member in enumerate(range(first_id, stop_id)):
        for local_level in range(depth_now):
            target = (member + 1 >> depth_now - local_level) - 1
            table[target, offset * depth_now + local_level] = 1.0
    return table


def solve_diagonal(residual, blocks):
    whole_blocks = lax.all_gather(blocks, "col", axis=1, tiled=True)
    whole_res = lax.all_gather(residual, "col", axis=1, tiled=True)
    rows_full = jnp.einsum(
        "nki,nkr->nir", whole_blocks, whole_res, preferred_element_type=jnp.float32
    )
    share = rows_full.shape[1] // lax.axis_size("col")
    owned = lax.dynamic_slice_in_dim(rows_full, lax.axis_index("col") * share, share, 1)
    return (owned, rows_full.astype(jnp.bfloat16))


def upper_sum(values):
    return lax.psum(values, "row")


def local(anc_lower, anc_upper, sub_lower, sub_upper, anc_rhs, sub_rhs, layer_subtree, sub_pattern):
    layers = lax.axis_size("gz")
    levels = layers.bit_length() - 1
    anc_count = layers - 1
    row_count = lax.axis_size("row")
    col_count = lax.axis_size("col")
    rows_here = anc_lower.shape[2]
    cols_here = anc_lower.shape[1]
    sub_start = [0]
    for member in range(SUB_NODES):
        sub_start.append(sub_start[-1] + levels + (member + 1).bit_length() - 1)
    anc_start = [0]
    for member in range(anc_count):
        anc_start.append(anc_start[-1] + (member + 1).bit_length() - 1)
    low_pattern = sub_pattern[:, 0].astype(jnp.float32)
    up_pattern = sub_pattern[:, 1].astype(jnp.float32)
    layer_here = lax.axis_index("gz")
    subtree = jnp.sum(
        jnp.where(jnp.arange(layers, dtype=jnp.int32) == layer_here, layer_subtree, 0)
    )
    powers = jnp.asarray(2 ** (levels - np.arange(levels)), jnp.int32)
    heap_ids = (subtree + layers) // powers - 1
    choose = (heap_ids[:, None] == jnp.arange(anc_count, dtype=jnp.int32)[None, :]).astype(
        jnp.float32
    )
    first_layer = (layer_here == 0).astype(jnp.float32)
    row_index = lax.axis_index("row")
    col_index = lax.axis_index("col")
    holds_piece = (row_index == col_index * row_count // col_count).astype(jnp.float32)
    piece_start = jnp.clip(col_index * cols_here - row_index * rows_here, 0, rows_here - cols_here)

    def own_piece(rows_block):
        return holds_piece * lax.dynamic_slice_in_dim(rows_block, piece_start, cols_here, 1).astype(
            jnp.float32
        )

    sub_acc = jnp.zeros((SUB_NODES, cols_here, R), jnp.float32)
    to_anc = jnp.zeros((anc_count, cols_here, R), jnp.float32)
    sub_rows = {}
    for depth_now in reversed(range(SUB_LEVELS)):
        first_id, stop_id = level_span(depth_now)
        node_count = stop_id - first_id
        given = sub_rhs[first_id:stop_id].astype(jnp.float32)
        if depth_now + 1 < SUB_LEVELS:
            given = given - lax.psum(sub_acc[first_id:stop_id], "row")
        unused, solved = solve_diagonal(given.astype(jnp.bfloat16), sub_lower[first_id:stop_id])
        sub_rows[depth_now] = solved
        per_node = levels + depth_now
        opening = SUB_NODES + sub_start[first_id]
        blocks = sub_lower[opening : opening + node_count * per_node].reshape(
            node_count, per_node, cols_here, rows_here
        )
        weights = low_pattern[sub_start[first_id] : sub_start[stop_id]].reshape(
            node_count, per_node
        )
        updates = jnp.einsum("npik,nkr->npir", blocks, solved, preferred_element_type=jnp.float32)
        updates = updates * weights[:, :, None, None]
        to_anc = to_anc + jnp.einsum("ea,eir->air", choose, jnp.sum(updates[:, :levels], 0))
        if depth_now > 0:
            table = jnp.asarray(local_routes(first_id, stop_id, depth_now, SUB_NODES))
            sub_acc = sub_acc + jnp.einsum(
                "tq,qir->tir", table, updates[:, levels:].reshape(-1, cols_here, R)
            )
    anc_acc = jnp.zeros((anc_count, cols_here, R), jnp.float32)
    anc_rows = {}
    for depth_now in reversed(range(levels)):
        first_id, stop_id = level_span(depth_now)
        node_count = stop_id - first_id
        joined = to_anc[first_id:stop_id] + first_layer * anc_acc[first_id:stop_id]
        reached = lax.psum(joined, ("gz", "row"))
        given = anc_rhs[first_id:stop_id].astype(jnp.float32) - reached
        unused, solved = solve_diagonal(given.astype(jnp.bfloat16), anc_lower[first_id:stop_id])
        anc_rows[depth_now] = solved
        if depth_now > 0:
            opening = anc_count + anc_start[first_id]
            blocks = anc_lower[opening : opening + node_count * depth_now].reshape(
                node_count, depth_now, cols_here, rows_here
            )
            updates = jnp.einsum(
                "npik,nkr->npir", blocks, solved, preferred_element_type=jnp.float32
            )
            table = jnp.asarray(local_routes(first_id, stop_id, depth_now, anc_count))
            anc_acc = anc_acc + jnp.einsum("tq,qir->tir", table, updates.reshape(-1, cols_here, R))
    anc_z_parts = []
    anc_out_parts = []
    for depth_now in range(levels):
        first_id, stop_id = level_span(depth_now)
        node_count = stop_id - first_id
        given = own_piece(anc_rows[depth_now])
        if depth_now > 0:
            z_sofar = jnp.concatenate(anc_z_parts, 0)
            table = local_routes(first_id, stop_id, depth_now, anc_count)[:first_id].T
            sources = jnp.einsum(
                "qa,akr->qkr",
                jnp.asarray(table, jnp.bfloat16),
                z_sofar,
                preferred_element_type=jnp.float32,
            )
            sources = sources.astype(jnp.bfloat16).reshape(node_count, depth_now, rows_here, R)
            opening = anc_count + anc_start[first_id]
            blocks = anc_upper[opening : opening + node_count * depth_now].reshape(
                node_count, depth_now, cols_here, rows_here
            )
            updates = jnp.einsum(
                "npik,npkr->npir", blocks, sources, preferred_element_type=jnp.float32
            )
            given = given - jnp.sum(updates, 1)
        summed = upper_sum(given)
        owned, solved = solve_diagonal(summed.astype(jnp.bfloat16), anc_upper[first_id:stop_id])
        anc_out_parts.append(owned)
        anc_z_parts.append(solved)
    anc_z_all = jnp.concatenate(anc_z_parts, 0)
    selected = jnp.einsum(
        "ea,akr->ekr", choose.astype(jnp.bfloat16), anc_z_all, preferred_element_type=jnp.float32
    )
    selected = selected.astype(jnp.bfloat16)
    sub_z_parts = []
    sub_out_parts = []
    for depth_now in range(SUB_LEVELS):
        first_id, stop_id = level_span(depth_now)
        node_count = stop_id - first_id
        per_node = levels + depth_now
        opening = SUB_NODES + sub_start[first_id]
        blocks = sub_upper[opening : opening + node_count * per_node].reshape(
            node_count, per_node, cols_here, rows_here
        )
        weights = up_pattern[sub_start[first_id] : sub_start[stop_id]].reshape(node_count, per_node)
        updates = jnp.einsum(
            "npik,pkr->npir", blocks[:, :levels], selected, preferred_element_type=jnp.float32
        )
        if depth_now > 0:
            z_sofar = sub_z_parts[0]
            table = local_routes(first_id, stop_id, depth_now, SUB_NODES)[:first_id].T
            sources = jnp.einsum(
                "qa,akr->qkr",
                jnp.asarray(table, jnp.bfloat16),
                z_sofar,
                preferred_element_type=jnp.float32,
            )
            sources = sources.astype(jnp.bfloat16).reshape(node_count, depth_now, rows_here, R)
            local_updates = jnp.einsum(
                "npik,npkr->npir", blocks[:, levels:], sources, preferred_element_type=jnp.float32
            )
            updates = jnp.concatenate([updates, local_updates], 1)
        change = jnp.sum(updates * weights[:, :, None, None], 1)
        summed = upper_sum(own_piece(sub_rows[depth_now]) - change)
        owned, solved = solve_diagonal(summed.astype(jnp.bfloat16), sub_upper[first_id:stop_id])
        sub_out_parts.append(owned)
        sub_z_parts.append(solved)
    return (jnp.concatenate(anc_out_parts, 0), jnp.concatenate(sub_out_parts, 0))


BF = jnp.bfloat16
F32 = jnp.float32
MESH = pl.DeviceIdType.MESH
HALVES = 2


def times(vectors, block):
    return jnp.dot(vectors, block, preferred_element_type=F32)


def times_t(vectors, block):
    return lax.dot_general(vectors, block, (((1,), (1,)), ((), ())), preferred_element_type=F32)


def fused_kernel(
    layers,
    rows_n,
    cols_n,
    anc_lower,
    anc_upper,
    sub_lower,
    sub_upper,
    anc_rhs,
    sub_rhs,
    layer_subtree,
    pattern,
    anc_out,
    sub_out,
    al,
    au,
    sl,
    su,
    ar,
    sr,
    pair_send,
    pair_recv,
    one_send,
    one_recv,
    all_send,
    all_recv,
    diag_recv,
    flipped,
    piece_send,
    piece_recv,
    load_sem,
    send_sem,
    recv_sem,
):
    gz = lax.axis_index("gz")
    row = lax.axis_index("row")
    col = lax.axis_index("col")
    loads = {}

    def load(name, source, target):
        copy = pltpu.make_async_copy(source, target, load_sem.at[len(loads)])
        copy.start()
        loads[name] = copy

    load("sr", sub_rhs, sr)
    load("e12", sub_lower.at[pl.ds(1, 2)], sl.at[pl.ds(1, 2)])
    load("low", sub_lower.at[pl.ds(3, 5)], sl.at[pl.ds(3, 5)])
    load("e0", sub_lower.at[0], sl.at[0])
    load("ar", anc_rhs, ar)
    load("al", anc_lower, al)
    load("au", anc_upper, au)
    load("su", sub_upper, su)

    def row_peer(j):
        return (gz, lax.rem(row + j, rows_n), col)

    def col_peer(j):
        return (gz, row, lax.rem(col + j, cols_n))

    barrier = pltpu.get_barrier_semaphore()
    peers = [row_peer(j) for j in range(1, rows_n)] + [col_peer(j) for j in range(1, cols_n)]
    wide = [
        (lax.rem(gz + g, layers), lax.rem(row + j, rows_n), col)
        for g in range(layers)
        for j in range(rows_n)
        if g or j
    ]
    peers = peers + wide[rows_n - 1 :]
    for peer in peers:
        pl.semaphore_signal(barrier, inc=1, device_id=peer, device_id_type=MESH)

    started = []
    half = sr.shape[1] // HALVES
    span = [slice(h * half, (h + 1) * half) for h in range(HALVES)]
    each = range(HALVES)

    def send(h, step, source, target, peer_list):
        made = []
        for j, peer in enumerate(peer_list):
            copy = pltpu.make_async_remote_copy(
                src_ref=source(j),
                dst_ref=target(j),
                send_sem=send_sem.at[h, step, j],
                recv_sem=recv_sem.at[h, step, j],
                device_id=peer,
                device_id_type=MESH,
            )
            copy.start()
            made.append(copy)
        started.extend(made)
        return made

    def begin(h, step, values, peer_list, send_buf, recv_buf):
        for n, value in enumerate(values):
            send_buf[h, n] = value.astype(BF)
        made = send(h, step, lambda j: send_buf.at[h], lambda j: recv_buf.at[h, j], peer_list)
        return h, list(values), made, recv_buf

    def finish(handle):
        h, sums, made, recv_buf = handle
        for j, copy in enumerate(made):
            copy.wait_recv()
            for n in range(len(sums)):
                sums[n] = sums[n] + recv_buf[h, j, n].astype(F32)
        return sums

    row_list = [row_peer(j) for j in range(1, rows_n)]
    col_list = [col_peer(j) for j in range(1, cols_n)]

    anc_here = jnp.where((layers + layer_subtree[gz]) // layers - 1 == 0, 1, 0)
    low = [pattern[0, p] for p in range(5)]
    up = [pattern[1, p] for p in range(5)]
    low = [(w * anc_here if p in (0, 1, 3) else w).astype(F32) for p, w in enumerate(low)]
    up = [(w * anc_here if p in (0, 1, 3) else w).astype(F32) for p, w in enumerate(up)]
    on_diag = jnp.where(row == col, 1.0, 0.0).astype(F32)

    loads["sr"].wait()
    loads["e12"].wait()
    parts = [[times(sr[m, span[h]], sl[m]) for m in (1, 2)] for h in each]
    pl.semaphore_wait(barrier, len(peers))
    step = [begin(h, 0, parts[h], col_list, pair_send.at[0], pair_recv.at[0]) for h in each]
    loads["low"].wait()
    y = [None] * HALVES
    for h in each:
        y[h] = [v.astype(BF) for v in finish(step[h])]
        change = low[2] * times_t(y[h][0], sl[5]) + low[4] * times_t(y[h][1], sl[7])
        step[h] = begin(h, 1, [change], row_list, one_send.at[0], one_recv.at[0])
    loads["e0"].wait()
    to_anc = [low[1] * times_t(y[h][0], sl[4]) + low[3] * times_t(y[h][1], sl[6]) for h in each]

    for h in each:
        r0 = (sr[0, span[h]].astype(F32) - finish(step[h])[0]).astype(BF)
        step[h] = begin(h, 2, [times(r0, sl[0])], col_list, one_send.at[1], one_recv.at[1])
    loads["ar"].wait()
    loads["al"].wait()
    for h in each:
        y0 = finish(step[h])[0].astype(BF)
        y[h] = [y0] + y[h]
        step[h] = begin(
            h, 3, [to_anc[h] + low[0] * times_t(y0, sl[3])], wide, all_send, all_recv
        )

    for h in each:
        ra = (ar[0, span[h]].astype(F32) - finish(step[h])[0]).astype(BF)
        part = times(ra, al[0])
        step[h] = part
        one_send[2, h, 0] = part.astype(BF)

        @pl.when(row != col)
        def to_diag():
            slot = lax.rem(col - row + cols_n - 1, cols_n)
            copy = pltpu.make_async_remote_copy(
                src_ref=one_send.at[2, h],
                dst_ref=one_recv.at[2, h, slot],
                send_sem=send_sem.at[h, 4, 0],
                recv_sem=recv_sem.at[h, 4, slot],
                device_id=(gz, row, row),
                device_id_type=MESH,
            )
            copy.start()

    for h in each:
        spread = [
            pltpu.make_async_remote_copy(
                src_ref=one_send.at[3, h],
                dst_ref=diag_recv.at[h],
                send_sem=send_sem.at[h, 5, j],
                recv_sem=recv_sem.at[h, 5, 0],
                device_id=peer,
                device_id_type=MESH,
            )
            for j, peer in enumerate(row_list)
        ]

        @pl.when(row == col)
        def at_diag():
            total = step[h]
            for j in range(cols_n - 1):
                pltpu.make_async_remote_copy(
                    src_ref=one_send.at[2, h],
                    dst_ref=one_recv.at[2, h, j],
                    send_sem=send_sem.at[h, 4, 0],
                    recv_sem=recv_sem.at[h, 4, j],
                    device_id=(gz, row, col),
                    device_id_type=MESH,
                ).wait_recv()
                total = total + one_recv[2, h, j, 0].astype(F32)
            one_send[3, h, 0] = total.astype(BF)
            for copy in spread:
                copy.start()
            diag_recv[h, 0] = total.astype(BF)

    loads["au"].wait()
    loads["su"].wait()
    for h in each:
        spread = [
            pltpu.make_async_remote_copy(
                src_ref=one_send.at[3, h],
                dst_ref=diag_recv.at[h],
                send_sem=send_sem.at[h, 5, j],
                recv_sem=recv_sem.at[h, 5, 0],
                device_id=peer,
                device_id_type=MESH,
            )
            for j, peer in enumerate(row_list)
        ]

        @pl.when(row == col)
        def sent_diag():
            for copy in spread:
                copy.wait_send()

        @pl.when(row != col)
        def off_diag():
            pltpu.make_async_remote_copy(
                src_ref=one_send.at[2, h],
                dst_ref=one_recv.at[2, h, 0],
                send_sem=send_sem.at[h, 4, 0],
                recv_sem=recv_sem.at[h, 4, 0],
                device_id=(gz, row, row),
                device_id_type=MESH,
            ).wait_send()
            spread[0].wait_recv()

        part = times(diag_recv[h, 0], au[0])
        step[h] = begin(h, 6, [part], col_list, one_send.at[4], one_recv.at[4])
    piece = sr.shape[2] // cols_n
    mine = pl.ds(pl.multiple_of(col * piece, piece), piece)

    za_full = [None] * HALVES
    za = [None] * HALVES
    for h in each:
        za_full[h] = finish(step[h])[0]
        za[h] = za_full[h].astype(BF)
        part = on_diag * y[h][0].astype(F32) - up[0] * times_t(za[h], su[3])
        step[h] = begin(h, 7, [part], row_list, one_send.at[5], one_recv.at[5])
    left = [
        [
            on_diag * y[h][1].astype(F32) - up[1] * times_t(za[h], su[4]),
            on_diag * y[h][2].astype(F32) - up[3] * times_t(za[h], su[6]),
        ]
        for h in each
    ]
    flipped[0] = jnp.transpose(jnp.concatenate(za_full, 0))
    anc_out[0] = flipped[0, mine, :]
    for h in each:
        t0 = finish(step[h])[0].astype(BF)
        step[h] = begin(h, 8, [times(t0, su[0])], col_list, one_send.at[6], one_recv.at[6])

    z0_full = [None] * HALVES
    for h in each:
        z0_full[h] = finish(step[h])[0]
        z0 = z0_full[h].astype(BF)
        s1 = left[h][0] - up[2] * times_t(z0, su[5])
        s2 = left[h][1] - up[4] * times_t(z0, su[7])
        step[h] = begin(h, 9, [s1, s2], row_list, pair_send.at[1], pair_recv.at[1])
    flipped[1] = jnp.transpose(jnp.concatenate(z0_full, 0))
    sub_out[0] = flipped[1, mine, :]
    for h in each:
        t1, t2 = finish(step[h])
        part1 = times(t1.astype(BF), su[1])
        part2 = times(t2.astype(BF), su[2])
        for c in range(cols_n):
            lanes = slice(c * piece, (c + 1) * piece)
            both = jnp.concatenate([part1[:, lanes], part2[:, lanes]], 1)
            piece_send[h, c] = both.astype(BF)
        step[h] = send(
            h,
            10,
            lambda j: piece_send.at[h, lax.rem(col + j + 1, cols_n)],
            lambda j: piece_recv.at[h, j],
            col_list,
        )
    totals = []
    for h in each:
        total = piece_send[h, col].astype(F32)
        for j, copy in enumerate(step[h]):
            copy.wait_recv()
            total = total + piece_recv[h, j].astype(F32)
        totals.append(total)
    total = jnp.transpose(jnp.concatenate(totals, 0))
    sub_out[1] = total[:piece]
    sub_out[2] = total[piece:]
    for copy in started:
        copy.wait_send()


def fused(mesh):
    layers, rows_n, cols_n = (mesh.shape[a] for a in ("gz", "row", "col"))

    def local_fused(*args):
        anc_lower, anc_upper, sub_lower, sub_upper, anc_rhs, sub_rhs, subtree, pattern = args
        cut, right = anc_rhs.shape[1], anc_rhs.shape[2]
        anc_rhs = jnp.swapaxes(anc_rhs, 1, 2)
        sub_rhs = jnp.swapaxes(sub_rhs, 1, 2)
        pattern = jnp.swapaxes(pattern, 0, 1)
        args = args[:4] + (anc_rhs, sub_rhs, subtree, pattern)
        piece = cut // cols_n
        vec = (right // HALVES, cut)
        H = HALVES
        peers_n = max(rows_n, cols_n) - 1
        hbm = pl.BlockSpec(memory_space=pl.ANY)
        smem = pl.BlockSpec(memory_space=pltpu.SMEM)
        vmem = pl.BlockSpec(memory_space=pltpu.VMEM)
        return pl.pallas_call(
            functools.partial(fused_kernel, layers, rows_n, cols_n),
            out_shape=(
                jax.ShapeDtypeStruct((1, piece, right), F32),
                jax.ShapeDtypeStruct((SUB_NODES, piece, right), F32),
            ),
            in_specs=[hbm] * 6 + [smem] * 2,
            out_specs=(vmem, vmem),
            scratch_shapes=[
                pltpu.VMEM(anc_lower.shape, BF),
                pltpu.VMEM(anc_upper.shape, BF),
                pltpu.VMEM(sub_lower.shape, BF),
                pltpu.VMEM(sub_upper.shape, BF),
                pltpu.VMEM(anc_rhs.shape, BF),
                pltpu.VMEM(sub_rhs.shape, BF),
                pltpu.VMEM((2, H, 2) + vec, BF),
                pltpu.VMEM((2, H, peers_n, 2) + vec, BF),
                pltpu.VMEM((7, H, 1) + vec, BF),
                pltpu.VMEM((7, H, peers_n, 1) + vec, BF),
                pltpu.VMEM((H, 1) + vec, BF),
                pltpu.VMEM((H, layers * rows_n - 1, 1) + vec, BF),
                pltpu.VMEM((H, 1) + vec, BF),
                pltpu.VMEM((2, cut, right), F32),
                pltpu.VMEM((H, cols_n, right // H, 2 * piece), BF),
                pltpu.VMEM((H, cols_n - 1, right // H, 2 * piece), BF),
                pltpu.SemaphoreType.DMA((8,)),
                pltpu.SemaphoreType.DMA((H, 11, layers * rows_n)),
                pltpu.SemaphoreType.DMA((H, 11, layers * rows_n)),
            ],
            compiler_params=pltpu.CompilerParams(collective_id=0, has_side_effects=True),
        )(*args)

    return local_fused


def solution(mesh):
    in_specs = (
        P(None, "col", "row"),
        P(None, "col", "row"),
        P("gz", "col", "row"),
        P("gz", "col", "row"),
        P(None, "col", None),
        P("gz", "col", None),
        P(),
        P("gz", None),
    )
    out_specs = (P(None, ("row", "col"), None), P("gz", ("row", "col"), None))
    one_anc = mesh.shape["gz"] == 2
    square = mesh.shape["row"] == mesh.shape["col"] == 4
    body = fused(mesh) if one_anc and square else local
    return jax.shard_map(body, mesh=mesh, in_specs=in_specs, out_specs=out_specs, check_vma=False)
```

```python
import functools

import jax
import jax.numpy as jnp
import numpy as np
from jax import lax
from jax.experimental import pallas as pl
from jax.experimental.pallas import tpu as pltpu
from jax.sharding import PartitionSpec as P

R = 64
SUB_LEVELS = 2
SUB_NODES = 3


def level_span(depth_now):
    return (2**depth_now - 1, 2 ** (depth_now + 1) - 1)


def local_routes(first_id, stop_id, depth_now, target_count):
    table = np.zeros((target_count, (stop_id - first_id) * depth_now), np.float32)
    for offset, member in enumerate(range(first_id, stop_id)):
        for local_level in range(depth_now):
            target = (member + 1 >> depth_now - local_level) - 1
            table[target, offset * depth_now + local_level] = 1.0
    return table


def solve_diagonal(residual, blocks):
    whole_blocks = lax.all_gather(blocks, "col", axis=1, tiled=True)
    whole_res = lax.all_gather(residual, "col", axis=1, tiled=True)
    rows_full = jnp.einsum(
        "nki,nkr->nir", whole_blocks, whole_res, preferred_element_type=jnp.float32
    )
    share = rows_full.shape[1] // lax.axis_size("col")
    owned = lax.dynamic_slice_in_dim(rows_full, lax.axis_index("col") * share, share, 1)
    return (owned, rows_full.astype(jnp.bfloat16))


def upper_sum(values):
    return lax.psum(values, "row")


def local(anc_lower, anc_upper, sub_lower, sub_upper, anc_rhs, sub_rhs, layer_subtree, sub_pattern):
    layers = lax.axis_size("gz")
    levels = layers.bit_length() - 1
    anc_count = layers - 1
    row_count = lax.axis_size("row")
    col_count = lax.axis_size("col")
    rows_here = anc_lower.shape[2]
    cols_here = anc_lower.shape[1]
    sub_start = [0]
    for member in range(SUB_NODES):
        sub_start.append(sub_start[-1] + levels + (member + 1).bit_length() - 1)
    anc_start = [0]
    for member in range(anc_count):
        anc_start.append(anc_start[-1] + (member + 1).bit_length() - 1)
    low_pattern = sub_pattern[:, 0].astype(jnp.float32)
    up_pattern = sub_pattern[:, 1].astype(jnp.float32)
    layer_here = lax.axis_index("gz")
    subtree = jnp.sum(
        jnp.where(jnp.arange(layers, dtype=jnp.int32) == layer_here, layer_subtree, 0)
    )
    powers = jnp.asarray(2 ** (levels - np.arange(levels)), jnp.int32)
    heap_ids = (subtree + layers) // powers - 1
    choose = (heap_ids[:, None] == jnp.arange(anc_count, dtype=jnp.int32)[None, :]).astype(
        jnp.float32
    )
    first_layer = (layer_here == 0).astype(jnp.float32)
    row_index = lax.axis_index("row")
    col_index = lax.axis_index("col")
    holds_piece = (row_index == col_index * row_count // col_count).astype(jnp.float32)
    piece_start = jnp.clip(col_index * cols_here - row_index * rows_here, 0, rows_here - cols_here)

    def own_piece(rows_block):
        return holds_piece * lax.dynamic_slice_in_dim(rows_block, piece_start, cols_here, 1).astype(
            jnp.float32
        )

    sub_acc = jnp.zeros((SUB_NODES, cols_here, R), jnp.float32)
    to_anc = jnp.zeros((anc_count, cols_here, R), jnp.float32)
    sub_rows = {}
    for depth_now in reversed(range(SUB_LEVELS)):
        first_id, stop_id = level_span(depth_now)
        node_count = stop_id - first_id
        given = sub_rhs[first_id:stop_id].astype(jnp.float32)
        if depth_now + 1 < SUB_LEVELS:
            given = given - lax.psum(sub_acc[first_id:stop_id], "row")
        unused, solved = solve_diagonal(given.astype(jnp.bfloat16), sub_lower[first_id:stop_id])
        sub_rows[depth_now] = solved
        per_node = levels + depth_now
        opening = SUB_NODES + sub_start[first_id]
        blocks = sub_lower[opening : opening + node_count * per_node].reshape(
            node_count, per_node, cols_here, rows_here
        )
        weights = low_pattern[sub_start[first_id] : sub_start[stop_id]].reshape(
            node_count, per_node
        )
        updates = jnp.einsum("npik,nkr->npir", blocks, solved, preferred_element_type=jnp.float32)
        updates = updates * weights[:, :, None, None]
        to_anc = to_anc + jnp.einsum("ea,eir->air", choose, jnp.sum(updates[:, :levels], 0))
        if depth_now > 0:
            table = jnp.asarray(local_routes(first_id, stop_id, depth_now, SUB_NODES))
            sub_acc = sub_acc + jnp.einsum(
                "tq,qir->tir", table, updates[:, levels:].reshape(-1, cols_here, R)
            )
    anc_acc = jnp.zeros((anc_count, cols_here, R), jnp.float32)
    anc_rows = {}
    for depth_now in reversed(range(levels)):
        first_id, stop_id = level_span(depth_now)
        node_count = stop_id - first_id
        joined = to_anc[first_id:stop_id] + first_layer * anc_acc[first_id:stop_id]
        reached = lax.psum(joined, ("gz", "row"))
        given = anc_rhs[first_id:stop_id].astype(jnp.float32) - reached
        unused, solved = solve_diagonal(given.astype(jnp.bfloat16), anc_lower[first_id:stop_id])
        anc_rows[depth_now] = solved
        if depth_now > 0:
            opening = anc_count + anc_start[first_id]
            blocks = anc_lower[opening : opening + node_count * depth_now].reshape(
                node_count, depth_now, cols_here, rows_here
            )
            updates = jnp.einsum(
                "npik,nkr->npir", blocks, solved, preferred_element_type=jnp.float32
            )
            table = jnp.asarray(local_routes(first_id, stop_id, depth_now, anc_count))
            anc_acc = anc_acc + jnp.einsum("tq,qir->tir", table, updates.reshape(-1, cols_here, R))
    anc_z_parts = []
    anc_out_parts = []
    for depth_now in range(levels):
        first_id, stop_id = level_span(depth_now)
        node_count = stop_id - first_id
        given = own_piece(anc_rows[depth_now])
        if depth_now > 0:
            z_sofar = jnp.concatenate(anc_z_parts, 0)
            table = local_routes(first_id, stop_id, depth_now, anc_count)[:first_id].T
            sources = jnp.einsum(
                "qa,akr->qkr",
                jnp.asarray(table, jnp.bfloat16),
                z_sofar,
                preferred_element_type=jnp.float32,
            )
            sources = sources.astype(jnp.bfloat16).reshape(node_count, depth_now, rows_here, R)
            opening = anc_count + anc_start[first_id]
            blocks = anc_upper[opening : opening + node_count * depth_now].reshape(
                node_count, depth_now, cols_here, rows_here
            )
            updates = jnp.einsum(
                "npik,npkr->npir", blocks, sources, preferred_element_type=jnp.float32
            )
            given = given - jnp.sum(updates, 1)
        summed = upper_sum(given)
        owned, solved = solve_diagonal(summed.astype(jnp.bfloat16), anc_upper[first_id:stop_id])
        anc_out_parts.append(owned)
        anc_z_parts.append(solved)
    anc_z_all = jnp.concatenate(anc_z_parts, 0)
    selected = jnp.einsum(
        "ea,akr->ekr", choose.astype(jnp.bfloat16), anc_z_all, preferred_element_type=jnp.float32
    )
    selected = selected.astype(jnp.bfloat16)
    sub_z_parts = []
    sub_out_parts = []
    for depth_now in range(SUB_LEVELS):
        first_id, stop_id = level_span(depth_now)
        node_count = stop_id - first_id
        per_node = levels + depth_now
        opening = SUB_NODES + sub_start[first_id]
        blocks = sub_upper[opening : opening + node_count * per_node].reshape(
            node_count, per_node, cols_here, rows_here
        )
        weights = up_pattern[sub_start[first_id] : sub_start[stop_id]].reshape(node_count, per_node)
        updates = jnp.einsum(
            "npik,pkr->npir", blocks[:, :levels], selected, preferred_element_type=jnp.float32
        )
        if depth_now > 0:
            z_sofar = sub_z_parts[0]
            table = local_routes(first_id, stop_id, depth_now, SUB_NODES)[:first_id].T
            sources = jnp.einsum(
                "qa,akr->qkr",
                jnp.asarray(table, jnp.bfloat16),
                z_sofar,
                preferred_element_type=jnp.float32,
            )
            sources = sources.astype(jnp.bfloat16).reshape(node_count, depth_now, rows_here, R)
            local_updates = jnp.einsum(
                "npik,npkr->npir", blocks[:, levels:], sources, preferred_element_type=jnp.float32
            )
            updates = jnp.concatenate([updates, local_updates], 1)
        change = jnp.sum(updates * weights[:, :, None, None], 1)
        summed = upper_sum(own_piece(sub_rows[depth_now]) - change)
        owned, solved = solve_diagonal(summed.astype(jnp.bfloat16), sub_upper[first_id:stop_id])
        sub_out_parts.append(owned)
        sub_z_parts.append(solved)
    return (jnp.concatenate(anc_out_parts, 0), jnp.concatenate(sub_out_parts, 0))


BF = jnp.bfloat16
F32 = jnp.float32
MESH = pl.DeviceIdType.MESH
HALVES = 2


def times(vectors, block):
    return jnp.dot(vectors, block, preferred_element_type=F32)


def times_t(vectors, block):
    return lax.dot_general(vectors, block, (((1,), (1,)), ((), ())), preferred_element_type=F32)


def fused_kernel(
    layers,
    rows_n,
    cols_n,
    anc_lower,
    anc_upper,
    sub_lower,
    sub_upper,
    anc_rhs,
    sub_rhs,
    layer_subtree,
    pattern,
    anc_out,
    sub_out,
    al,
    au,
    sl,
    su,
    ar,
    sr,
    pair_send,
    pair_recv,
    one_send,
    one_recv,
    all_send,
    all_recv,
    product_send,
    product_recv,
    flipped,
    piece_send,
    piece_recv,
    load_sem,
    send_sem,
    recv_sem,
):
    gz = lax.axis_index("gz")
    row = lax.axis_index("row")
    col = lax.axis_index("col")
    loads = {}

    def load(name, source, target):
        copy = pltpu.make_async_copy(source, target, load_sem.at[len(loads)])
        copy.start()
        loads[name] = copy

    load("sr", sub_rhs, sr)
    load("e12", sub_lower.at[pl.ds(1, 2)], sl.at[pl.ds(1, 2)])
    load("low", sub_lower.at[pl.ds(3, 5)], sl.at[pl.ds(3, 5)])
    load("e0", sub_lower.at[0], sl.at[0])
    load("ar", anc_rhs, ar)
    width = au.shape[2]
    load("al", anc_lower, al.at[pl.ds(0, 1)])
    load(
        "au",
        anc_upper.at[:, :, pl.ds(pl.multiple_of(gz * width, width), width)],
        au.at[pl.ds(0, 1)],
    )
    load("su", sub_upper, su)

    def row_peer(j):
        return (gz, lax.rem(row + j, rows_n), col)

    def col_peer(j):
        return (gz, row, lax.rem(col + j, cols_n))

    barrier = pltpu.get_barrier_semaphore()
    peers = [row_peer(j) for j in range(1, rows_n)] + [col_peer(j) for j in range(1, cols_n)]
    wide = [
        (lax.rem(gz + g, layers), lax.rem(row + j, rows_n), col)
        for g in range(layers)
        for j in range(rows_n)
        if g or j
    ]
    peers = peers + wide[rows_n - 1 :]
    for peer in peers:
        pl.semaphore_signal(barrier, inc=1, device_id=peer, device_id_type=MESH)

    started = []
    half = sr.shape[1] // HALVES
    span = [slice(h * half, (h + 1) * half) for h in range(HALVES)]
    each = range(HALVES)

    def send(h, step, source, target, peer_list):
        made = []
        for j, peer in enumerate(peer_list):
            copy = pltpu.make_async_remote_copy(
                src_ref=source(j),
                dst_ref=target(j),
                send_sem=send_sem.at[h, step, j],
                recv_sem=recv_sem.at[h, step, j],
                device_id=peer,
                device_id_type=MESH,
            )
            copy.start()
            made.append(copy)
        started.extend(made)
        return made

    def begin(h, step, values, peer_list, send_buf, recv_buf):
        for n, value in enumerate(values):
            send_buf[h, n] = value.astype(BF)
        made = send(h, step, lambda j: send_buf.at[h], lambda j: recv_buf.at[h, j], peer_list)
        return h, list(values), made, recv_buf

    def finish(handle):
        h, sums, made, recv_buf = handle
        for j, copy in enumerate(made):
            copy.wait_recv()
            for n in range(len(sums)):
                sums[n] = sums[n] + recv_buf[h, j, n].astype(F32)
        return sums

    row_list = [row_peer(j) for j in range(1, rows_n)]
    col_list = [col_peer(j) for j in range(1, cols_n)]

    anc_here = jnp.where((layers + layer_subtree[gz]) // layers - 1 == 0, 1, 0)
    low = [pattern[0, p] for p in range(5)]
    up = [pattern[1, p] for p in range(5)]
    low = [(w * anc_here if p in (0, 1, 3) else w).astype(F32) for p, w in enumerate(low)]
    up = [(w * anc_here if p in (0, 1, 3) else w).astype(F32) for p, w in enumerate(up)]
    on_diag = jnp.where(row == col, 1.0, 0.0).astype(F32)

    loads["sr"].wait()
    loads["e12"].wait()
    parts = [[times(sr[m, span[h]], sl[m]) for m in (1, 2)] for h in each]
    pl.semaphore_wait(barrier, len(peers))
    step = [begin(h, 0, parts[h], col_list, pair_send.at[0], pair_recv.at[0]) for h in each]

    loads["al"].wait()
    loads["au"].wait()
    blocks = send(0, 4, lambda j: al.at[0], lambda j: al.at[j + 1], row_list)
    blocks = blocks + send(0, 5, lambda j: au.at[0], lambda j: au.at[j + 1], col_list)
    loads["low"].wait()
    y = [None] * HALVES
    for h in each:
        y[h] = [v.astype(BF) for v in finish(step[h])]
        change = low[2] * times_t(y[h][0], sl[5]) + low[4] * times_t(y[h][1], sl[7])
        step[h] = begin(h, 1, [change], row_list, one_send.at[0], one_recv.at[0])
    loads["e0"].wait()
    to_anc = [low[1] * times_t(y[h][0], sl[4]) + low[3] * times_t(y[h][1], sl[6]) for h in each]

    for h in each:
        r0 = (sr[0, span[h]].astype(F32) - finish(step[h])[0]).astype(BF)
        step[h] = begin(h, 2, [times(r0, sl[0])], col_list, one_send.at[1], one_recv.at[1])
    loads["ar"].wait()
    for copy in blocks:
        copy.wait_recv()
    product = jnp.zeros((al.shape[1], width), F32)
    for b in range(rows_n):
        product = product + times(
            al[lax.rem(row - b + rows_n, rows_n)], au[lax.rem(col - b + cols_n, cols_n)]
        )
    product_send[0] = product.astype(BF)
    product_recv[0] = product.astype(BF)
    layer_list = [(lax.rem(gz + g, layers), row, col) for g in range(1, layers)]
    blocks = send(
        0, 11, lambda j: product_send.at[0], lambda j: product_recv.at[j + 1], layer_list
    )
    for h in each:
        y0 = finish(step[h])[0].astype(BF)
        y[h] = [y0] + y[h]
        step[h] = begin(
            h, 3, [to_anc[h] + low[0] * times_t(y0, sl[3])], wide, all_send, all_recv
        )

    for copy in blocks:
        copy.wait_recv()
    whole = jnp.concatenate(
        [product_recv[lax.rem(gz - g + layers, layers)] for g in range(layers)], 1
    )
    for h in each:
        ra = (ar[0, span[h]].astype(F32) - finish(step[h])[0]).astype(BF)
        step[h] = begin(h, 6, [times(ra, whole)], col_list, one_send.at[4], one_recv.at[4])
    loads["su"].wait()
    piece = sr.shape[2] // cols_n
    mine = pl.ds(pl.multiple_of(col * piece, piece), piece)

    za_full = [None] * HALVES
    za = [None] * HALVES
    for h in each:
        za_full[h] = finish(step[h])[0]
        za[h] = za_full[h].astype(BF)
        part = on_diag * y[h][0].astype(F32) - up[0] * times_t(za[h], su[3])
        step[h] = begin(h, 7, [part], row_list, one_send.at[5], one_recv.at[5])
    left = [
        [
            on_diag * y[h][1].astype(F32) - up[1] * times_t(za[h], su[4]),
            on_diag * y[h][2].astype(F32) - up[3] * times_t(za[h], su[6]),
        ]
        for h in each
    ]
    flipped[0] = jnp.transpose(jnp.concatenate(za_full, 0))
    anc_out[0] = flipped[0, mine, :]
    for h in each:
        t0 = finish(step[h])[0].astype(BF)
        step[h] = begin(h, 8, [times(t0, su[0])], col_list, one_send.at[6], one_recv.at[6])

    z0_full = [None] * HALVES
    for h in each:
        z0_full[h] = finish(step[h])[0]
        z0 = z0_full[h].astype(BF)
        s1 = left[h][0] - up[2] * times_t(z0, su[5])
        s2 = left[h][1] - up[4] * times_t(z0, su[7])
        step[h] = begin(h, 9, [s1, s2], row_list, pair_send.at[1], pair_recv.at[1])
    flipped[1] = jnp.transpose(jnp.concatenate(z0_full, 0))
    sub_out[0] = flipped[1, mine, :]
    for h in each:
        t1, t2 = finish(step[h])
        part1 = times(t1.astype(BF), su[1])
        part2 = times(t2.astype(BF), su[2])
        for c in range(cols_n):
            lanes = slice(c * piece, (c + 1) * piece)
            both = jnp.concatenate([part1[:, lanes], part2[:, lanes]], 1)
            piece_send[h, c] = both.astype(BF)
        step[h] = send(
            h,
            10,
            lambda j: piece_send.at[h, lax.rem(col + j + 1, cols_n)],
            lambda j: piece_recv.at[h, j],
            col_list,
        )
    totals = []
    for h in each:
        total = piece_send[h, col].astype(F32)
        for j, copy in enumerate(step[h]):
            copy.wait_recv()
            total = total + piece_recv[h, j].astype(F32)
        totals.append(total)
    total = jnp.transpose(jnp.concatenate(totals, 0))
    sub_out[1] = total[:piece]
    sub_out[2] = total[piece:]
    for copy in started:
        copy.wait_send()


def fused(mesh):
    layers, rows_n, cols_n = (mesh.shape[a] for a in ("gz", "row", "col"))

    def local_fused(*args):
        anc_lower, anc_upper, sub_lower, sub_upper, anc_rhs, sub_rhs, subtree, pattern = args
        cut, right = anc_rhs.shape[1], anc_rhs.shape[2]
        anc_rhs = jnp.swapaxes(anc_rhs, 1, 2)
        sub_rhs = jnp.swapaxes(sub_rhs, 1, 2)
        pattern = jnp.swapaxes(pattern, 0, 1)
        args = args[:4] + (anc_rhs, sub_rhs, subtree, pattern)
        piece = cut // cols_n
        vec = (right // HALVES, cut)
        H = HALVES
        peers_n = max(rows_n, cols_n) - 1
        hbm = pl.BlockSpec(memory_space=pl.ANY)
        smem = pl.BlockSpec(memory_space=pltpu.SMEM)
        vmem = pl.BlockSpec(memory_space=pltpu.VMEM)
        return pl.pallas_call(
            functools.partial(fused_kernel, layers, rows_n, cols_n),
            out_shape=(
                pltpu.VMEM((1, piece, right), F32),
                pltpu.VMEM((SUB_NODES, piece, right), F32),
            ),
            in_specs=[hbm] * 6 + [smem] * 2,
            out_specs=(vmem, vmem),
            scratch_shapes=[
                pltpu.VMEM((rows_n, cut, cut), BF),
                pltpu.VMEM((cols_n, cut, cut // layers), BF),
                pltpu.VMEM(sub_lower.shape, BF),
                pltpu.VMEM(sub_upper.shape, BF),
                pltpu.VMEM(anc_rhs.shape, BF),
                pltpu.VMEM(sub_rhs.shape, BF),
                pltpu.VMEM((2, H, 2) + vec, BF),
                pltpu.VMEM((2, H, peers_n, 2) + vec, BF),
                pltpu.VMEM((7, H, 1) + vec, BF),
                pltpu.VMEM((7, H, peers_n, 1) + vec, BF),
                pltpu.VMEM((H, 1) + vec, BF),
                pltpu.VMEM((H, layers * rows_n - 1, 1) + vec, BF),
                pltpu.VMEM((1, cut, cut // layers), BF),
                pltpu.VMEM((layers, cut, cut // layers), BF),
                pltpu.VMEM((2, cut, right), F32),
                pltpu.VMEM((H, cols_n, right // H, 2 * piece), BF),
                pltpu.VMEM((H, cols_n - 1, right // H, 2 * piece), BF),
                pltpu.SemaphoreType.DMA((8,)),
                pltpu.SemaphoreType.DMA((H, 12, layers * rows_n)),
                pltpu.SemaphoreType.DMA((H, 12, layers * rows_n)),
            ],
            compiler_params=pltpu.CompilerParams(collective_id=0, has_side_effects=True),
        )(*args)

    return local_fused


def solution(mesh):
    in_specs = (
        P(None, "col", "row"),
        P(None, "col", "row"),
        P("gz", "col", "row"),
        P("gz", "col", "row"),
        P(None, "col", None),
        P("gz", "col", None),
        P(),
        P("gz", None),
    )
    out_specs = (P(None, ("row", "col"), None), P("gz", ("row", "col"), None))
    one_anc = mesh.shape["gz"] == 2
    square = mesh.shape["row"] == mesh.shape["col"] == 4
    body = fused(mesh) if one_anc and square else local
    return jax.shard_map(body, mesh=mesh, in_specs=in_specs, out_specs=out_specs, check_vma=False)
```

```python
import functools

import jax
import jax.numpy as jnp
import numpy as np
from jax import lax
from jax.experimental import pallas as pl
from jax.experimental.pallas import tpu as pltpu
from jax.sharding import PartitionSpec as P

R = 64
SUB_LEVELS = 2
SUB_NODES = 3


def level_span(depth_now):
    return (2**depth_now - 1, 2 ** (depth_now + 1) - 1)


def local_routes(first_id, stop_id, depth_now, target_count):
    table = np.zeros((target_count, (stop_id - first_id) * depth_now), np.float32)
    for offset, member in enumerate(range(first_id, stop_id)):
        for local_level in range(depth_now):
            target = (member + 1 >> depth_now - local_level) - 1
            table[target, offset * depth_now + local_level] = 1.0
    return table


def solve_diagonal(residual, blocks):
    whole_blocks = lax.all_gather(blocks, "col", axis=1, tiled=True)
    whole_res = lax.all_gather(residual, "col", axis=1, tiled=True)
    rows_full = jnp.einsum(
        "nki,nkr->nir", whole_blocks, whole_res, preferred_element_type=jnp.float32
    )
    share = rows_full.shape[1] // lax.axis_size("col")
    owned = lax.dynamic_slice_in_dim(rows_full, lax.axis_index("col") * share, share, 1)
    return (owned, rows_full.astype(jnp.bfloat16))


def upper_sum(values):
    return lax.psum(values, "row")


def local(anc_lower, anc_upper, sub_lower, sub_upper, anc_rhs, sub_rhs, layer_subtree, sub_pattern):
    layers = lax.axis_size("gz")
    levels = layers.bit_length() - 1
    anc_count = layers - 1
    row_count = lax.axis_size("row")
    col_count = lax.axis_size("col")
    rows_here = anc_lower.shape[2]
    cols_here = anc_lower.shape[1]
    sub_start = [0]
    for member in range(SUB_NODES):
        sub_start.append(sub_start[-1] + levels + (member + 1).bit_length() - 1)
    anc_start = [0]
    for member in range(anc_count):
        anc_start.append(anc_start[-1] + (member + 1).bit_length() - 1)
    low_pattern = sub_pattern[:, 0].astype(jnp.float32)
    up_pattern = sub_pattern[:, 1].astype(jnp.float32)
    layer_here = lax.axis_index("gz")
    subtree = jnp.sum(
        jnp.where(jnp.arange(layers, dtype=jnp.int32) == layer_here, layer_subtree, 0)
    )
    powers = jnp.asarray(2 ** (levels - np.arange(levels)), jnp.int32)
    heap_ids = (subtree + layers) // powers - 1
    choose = (heap_ids[:, None] == jnp.arange(anc_count, dtype=jnp.int32)[None, :]).astype(
        jnp.float32
    )
    first_layer = (layer_here == 0).astype(jnp.float32)
    row_index = lax.axis_index("row")
    col_index = lax.axis_index("col")
    holds_piece = (row_index == col_index * row_count // col_count).astype(jnp.float32)
    piece_start = jnp.clip(col_index * cols_here - row_index * rows_here, 0, rows_here - cols_here)

    def own_piece(rows_block):
        return holds_piece * lax.dynamic_slice_in_dim(rows_block, piece_start, cols_here, 1).astype(
            jnp.float32
        )

    sub_acc = jnp.zeros((SUB_NODES, cols_here, R), jnp.float32)
    to_anc = jnp.zeros((anc_count, cols_here, R), jnp.float32)
    sub_rows = {}
    for depth_now in reversed(range(SUB_LEVELS)):
        first_id, stop_id = level_span(depth_now)
        node_count = stop_id - first_id
        given = sub_rhs[first_id:stop_id].astype(jnp.float32)
        if depth_now + 1 < SUB_LEVELS:
            given = given - lax.psum(sub_acc[first_id:stop_id], "row")
        unused, solved = solve_diagonal(given.astype(jnp.bfloat16), sub_lower[first_id:stop_id])
        sub_rows[depth_now] = solved
        per_node = levels + depth_now
        opening = SUB_NODES + sub_start[first_id]
        blocks = sub_lower[opening : opening + node_count * per_node].reshape(
            node_count, per_node, cols_here, rows_here
        )
        weights = low_pattern[sub_start[first_id] : sub_start[stop_id]].reshape(
            node_count, per_node
        )
        updates = jnp.einsum("npik,nkr->npir", blocks, solved, preferred_element_type=jnp.float32)
        updates = updates * weights[:, :, None, None]
        to_anc = to_anc + jnp.einsum("ea,eir->air", choose, jnp.sum(updates[:, :levels], 0))
        if depth_now > 0:
            table = jnp.asarray(local_routes(first_id, stop_id, depth_now, SUB_NODES))
            sub_acc = sub_acc + jnp.einsum(
                "tq,qir->tir", table, updates[:, levels:].reshape(-1, cols_here, R)
            )
    anc_acc = jnp.zeros((anc_count, cols_here, R), jnp.float32)
    anc_rows = {}
    for depth_now in reversed(range(levels)):
        first_id, stop_id = level_span(depth_now)
        node_count = stop_id - first_id
        joined = to_anc[first_id:stop_id] + first_layer * anc_acc[first_id:stop_id]
        reached = lax.psum(joined, ("gz", "row"))
        given = anc_rhs[first_id:stop_id].astype(jnp.float32) - reached
        unused, solved = solve_diagonal(given.astype(jnp.bfloat16), anc_lower[first_id:stop_id])
        anc_rows[depth_now] = solved
        if depth_now > 0:
            opening = anc_count + anc_start[first_id]
            blocks = anc_lower[opening : opening + node_count * depth_now].reshape(
                node_count, depth_now, cols_here, rows_here
            )
            updates = jnp.einsum(
                "npik,nkr->npir", blocks, solved, preferred_element_type=jnp.float32
            )
            table = jnp.asarray(local_routes(first_id, stop_id, depth_now, anc_count))
            anc_acc = anc_acc + jnp.einsum("tq,qir->tir", table, updates.reshape(-1, cols_here, R))
    anc_z_parts = []
    anc_out_parts = []
    for depth_now in range(levels):
        first_id, stop_id = level_span(depth_now)
        node_count = stop_id - first_id
        given = own_piece(anc_rows[depth_now])
        if depth_now > 0:
            z_sofar = jnp.concatenate(anc_z_parts, 0)
            table = local_routes(first_id, stop_id, depth_now, anc_count)[:first_id].T
            sources = jnp.einsum(
                "qa,akr->qkr",
                jnp.asarray(table, jnp.bfloat16),
                z_sofar,
                preferred_element_type=jnp.float32,
            )
            sources = sources.astype(jnp.bfloat16).reshape(node_count, depth_now, rows_here, R)
            opening = anc_count + anc_start[first_id]
            blocks = anc_upper[opening : opening + node_count * depth_now].reshape(
                node_count, depth_now, cols_here, rows_here
            )
            updates = jnp.einsum(
                "npik,npkr->npir", blocks, sources, preferred_element_type=jnp.float32
            )
            given = given - jnp.sum(updates, 1)
        summed = upper_sum(given)
        owned, solved = solve_diagonal(summed.astype(jnp.bfloat16), anc_upper[first_id:stop_id])
        anc_out_parts.append(owned)
        anc_z_parts.append(solved)
    anc_z_all = jnp.concatenate(anc_z_parts, 0)
    selected = jnp.einsum(
        "ea,akr->ekr", choose.astype(jnp.bfloat16), anc_z_all, preferred_element_type=jnp.float32
    )
    selected = selected.astype(jnp.bfloat16)
    sub_z_parts = []
    sub_out_parts = []
    for depth_now in range(SUB_LEVELS):
        first_id, stop_id = level_span(depth_now)
        node_count = stop_id - first_id
        per_node = levels + depth_now
        opening = SUB_NODES + sub_start[first_id]
        blocks = sub_upper[opening : opening + node_count * per_node].reshape(
            node_count, per_node, cols_here, rows_here
        )
        weights = up_pattern[sub_start[first_id] : sub_start[stop_id]].reshape(node_count, per_node)
        updates = jnp.einsum(
            "npik,pkr->npir", blocks[:, :levels], selected, preferred_element_type=jnp.float32
        )
        if depth_now > 0:
            z_sofar = sub_z_parts[0]
            table = local_routes(first_id, stop_id, depth_now, SUB_NODES)[:first_id].T
            sources = jnp.einsum(
                "qa,akr->qkr",
                jnp.asarray(table, jnp.bfloat16),
                z_sofar,
                preferred_element_type=jnp.float32,
            )
            sources = sources.astype(jnp.bfloat16).reshape(node_count, depth_now, rows_here, R)
            local_updates = jnp.einsum(
                "npik,npkr->npir", blocks[:, levels:], sources, preferred_element_type=jnp.float32
            )
            updates = jnp.concatenate([updates, local_updates], 1)
        change = jnp.sum(updates * weights[:, :, None, None], 1)
        summed = upper_sum(own_piece(sub_rows[depth_now]) - change)
        owned, solved = solve_diagonal(summed.astype(jnp.bfloat16), sub_upper[first_id:stop_id])
        sub_out_parts.append(owned)
        sub_z_parts.append(solved)
    return (jnp.concatenate(anc_out_parts, 0), jnp.concatenate(sub_out_parts, 0))


BF = jnp.bfloat16
F32 = jnp.float32
MESH = pl.DeviceIdType.MESH
HALVES = 2


def times(vectors, block):
    return jnp.dot(vectors, block, preferred_element_type=F32)


def times_t(vectors, block):
    return lax.dot_general(vectors, block, (((1,), (1,)), ((), ())), preferred_element_type=F32)


def fused_kernel(
    layers,
    rows_n,
    cols_n,
    anc_lower,
    anc_upper,
    sub_lower,
    sub_upper,
    anc_rhs,
    sub_rhs,
    layer_subtree,
    pattern,
    anc_out,
    sub_out,
    al,
    au,
    sl,
    su,
    ar,
    sr,
    pair_send,
    pair_recv,
    one_send,
    one_recv,
    all_send,
    all_recv,
    product_send,
    product_recv,
    flipped,
    piece_send,
    piece_recv,
    load_sem,
    send_sem,
    recv_sem,
):
    gz = lax.axis_index("gz")
    row = lax.axis_index("row")
    col = lax.axis_index("col")
    def row_peer(j):
        return (gz, lax.rem(row + j, rows_n), col)

    def col_peer(j):
        return (gz, row, lax.rem(col + j, cols_n))

    barrier = pltpu.get_barrier_semaphore()
    peers = [row_peer(j) for j in range(1, rows_n)] + [col_peer(j) for j in range(1, cols_n)]
    wide = [
        (lax.rem(gz + g, layers), lax.rem(row + j, rows_n), col)
        for g in range(layers)
        for j in range(rows_n)
        if g or j
    ]
    peers = peers + wide[rows_n - 1 :]
    for peer in peers:
        pl.semaphore_signal(barrier, inc=1, device_id=peer, device_id_type=MESH)

    loads = {}

    def load(name, source, target):
        copy = pltpu.make_async_copy(source, target, load_sem.at[len(loads)])
        copy.start()
        loads[name] = copy

    load("sr", sub_rhs, sr)
    load("e12", sub_lower.at[pl.ds(1, 2)], sl.at[pl.ds(1, 2)])
    load("low", sub_lower.at[pl.ds(3, 5)], sl.at[pl.ds(3, 5)])
    load("e0", sub_lower.at[0], sl.at[0])
    load("ar", anc_rhs, ar)
    width = au.shape[2]
    load("al", anc_lower, al.at[pl.ds(0, 1)])
    load(
        "au",
        anc_upper.at[:, :, pl.ds(pl.multiple_of(gz * width, width), width)],
        au.at[pl.ds(0, 1)],
    )
    load("su", sub_upper, su)

    started = []
    half = sr.shape[1] // HALVES
    span = [slice(h * half, (h + 1) * half) for h in range(HALVES)]
    each = range(HALVES)

    def send(h, step, source, target, peer_list):
        made = []
        for j, peer in enumerate(peer_list):
            copy = pltpu.make_async_remote_copy(
                src_ref=source(j),
                dst_ref=target(j),
                send_sem=send_sem.at[h, step, j],
                recv_sem=recv_sem.at[h, step, j],
                device_id=peer,
                device_id_type=MESH,
            )
            copy.start()
            made.append(copy)
        started.extend(made)
        return made

    def begin(h, step, values, peer_list, send_buf, recv_buf):
        for n, value in enumerate(values):
            send_buf[h, n] = value.astype(BF)
        made = send(h, step, lambda j: send_buf.at[h], lambda j: recv_buf.at[h, j], peer_list)
        return h, list(values), made, recv_buf

    def finish(handle):
        h, sums, made, recv_buf = handle
        for j, copy in enumerate(made):
            copy.wait_recv()
            for n in range(len(sums)):
                sums[n] = sums[n] + recv_buf[h, j, n].astype(F32)
        return sums

    row_list = [row_peer(j) for j in range(1, rows_n)]
    col_list = [col_peer(j) for j in range(1, cols_n)]

    anc_here = jnp.where((layers + layer_subtree[gz]) // layers - 1 == 0, 1, 0)
    low = [pattern[0, p] for p in range(5)]
    up = [pattern[1, p] for p in range(5)]
    low = [(w * anc_here if p in (0, 1, 3) else w).astype(F32) for p, w in enumerate(low)]
    up = [(w * anc_here if p in (0, 1, 3) else w).astype(F32) for p, w in enumerate(up)]
    on_diag = jnp.where(row == col, 1.0, 0.0).astype(F32)

    loads["sr"].wait()
    loads["e12"].wait()
    parts = [[times(sr[m, span[h]], sl[m]) for m in (1, 2)] for h in each]
    pl.semaphore_wait(barrier, len(peers))
    step = [begin(h, 0, parts[h], col_list, pair_send.at[0], pair_recv.at[0]) for h in each]

    loads["al"].wait()
    loads["au"].wait()
    blocks = send(0, 4, lambda j: al.at[0], lambda j: al.at[j + 1], row_list)

    def hop(right, stage):
        step_id = 5 if right else 10
        to = col + 1 if right else col + cols_n - 1
        copy = pltpu.make_async_remote_copy(
            src_ref=au.at[stage - 1 if right else (cols_n - stage + 1) % cols_n],
            dst_ref=au.at[stage if right else cols_n - stage],
            send_sem=send_sem.at[0, step_id, cols_n + stage - 1],
            recv_sem=recv_sem.at[0, step_id, cols_n + stage - 1],
            device_id=(gz, row, lax.rem(to, cols_n)),
            device_id_type=MESH,
        )
        if right:
            return copy, (col + 1 < cols_n) & (col >= stage - 1), col >= stage
        return copy, (col >= 1) & (col < cols_n - stage + 1), col < cols_n - stage

    def relay(stage):
        for right in (True, False):
            if stage > 1:
                before, unused, gets = hop(right, stage - 1)

                @pl.when(gets)
                def arrived():
                    before.wait_recv()

            if stage < cols_n:
                copy, sends, unused = hop(right, stage)

                @pl.when(sends)
                def forward():
                    copy.start()

    relay(1)
    loads["low"].wait()
    y = [None] * HALVES
    for h in each:
        y[h] = [v.astype(BF) for v in finish(step[h])]
        change = low[2] * times_t(y[h][0], sl[5]) + low[4] * times_t(y[h][1], sl[7])
        step[h] = begin(h, 1, [change], row_list, one_send.at[0], one_recv.at[0])
    for stage in range(2, cols_n - 1):
        relay(stage)
    loads["e0"].wait()
    to_anc = [low[1] * times_t(y[h][0], sl[4]) + low[3] * times_t(y[h][1], sl[6]) for h in each]

    for h in each:
        r0 = (sr[0, span[h]].astype(F32) - finish(step[h])[0]).astype(BF)
        step[h] = begin(h, 2, [times(r0, sl[0])], col_list, one_send.at[1], one_recv.at[1])
    relay(cols_n - 1)
    loads["ar"].wait()
    for h in each:
        y0 = finish(step[h])[0].astype(BF)
        y[h] = [y0] + y[h]
        step[h] = begin(
            h, 3, [to_anc[h] + low[0] * times_t(y0, sl[3])], wide, all_send, all_recv
        )
    relay(cols_n)
    for copy in blocks:
        copy.wait_recv()
    product = jnp.zeros((al.shape[1], width), F32)
    for b in range(rows_n):
        product = product + times(
            al[lax.rem(row - b + rows_n, rows_n)], au[lax.rem(col - b + cols_n, cols_n)]
        )
    product_send[0] = product.astype(BF)
    product_recv[0] = product.astype(BF)
    layer_list = [(lax.rem(gz + g, layers), row, col) for g in range(1, layers)]
    blocks = send(
        0, 11, lambda j: product_send.at[0], lambda j: product_recv.at[j + 1], layer_list
    )

    for copy in blocks:
        copy.wait_recv()
    whole = jnp.concatenate(
        [product_recv[lax.rem(gz - g + layers, layers)] for g in range(layers)], 1
    )
    for h in each:
        ra = (ar[0, span[h]].astype(F32) - finish(step[h])[0]).astype(BF)
        step[h] = begin(h, 6, [times(ra, whole)], col_list, one_send.at[4], one_recv.at[4])
    loads["su"].wait()
    piece = sr.shape[2] // cols_n
    mine = pl.ds(pl.multiple_of(col * piece, piece), piece)

    za_full = [None] * HALVES
    za = [None] * HALVES
    for h in each:
        za_full[h] = finish(step[h])[0]
        za[h] = za_full[h].astype(BF)
        part = on_diag * y[h][0].astype(F32) - up[0] * times_t(za[h], su[3])
        step[h] = begin(h, 7, [part], row_list, one_send.at[5], one_recv.at[5])
    left = [
        [
            on_diag * y[h][1].astype(F32) - up[1] * times_t(za[h], su[4]),
            on_diag * y[h][2].astype(F32) - up[3] * times_t(za[h], su[6]),
        ]
        for h in each
    ]
    flipped[0] = jnp.transpose(jnp.concatenate(za_full, 0))
    anc_out[0] = flipped[0, mine, :]
    for h in each:
        t0 = finish(step[h])[0].astype(BF)
        step[h] = begin(h, 8, [times(t0, su[0])], col_list, one_send.at[6], one_recv.at[6])

    z0_full = [None] * HALVES
    for h in each:
        z0_full[h] = finish(step[h])[0]
        z0 = z0_full[h].astype(BF)
        s1 = left[h][0] - up[2] * times_t(z0, su[5])
        s2 = left[h][1] - up[4] * times_t(z0, su[7])
        step[h] = begin(h, 9, [s1, s2], row_list, pair_send.at[1], pair_recv.at[1])
    flipped[1] = jnp.transpose(jnp.concatenate(z0_full, 0))
    sub_out[0] = flipped[1, mine, :]
    for h in each:
        t1, t2 = finish(step[h])
        part1 = times(t1.astype(BF), su[1])
        part2 = times(t2.astype(BF), su[2])
        for c in range(cols_n):
            lanes = slice(c * piece, (c + 1) * piece)
            both = jnp.concatenate([part1[:, lanes], part2[:, lanes]], 1)
            piece_send[h, c] = both.astype(BF)
        step[h] = send(
            h,
            10,
            lambda j: piece_send.at[h, lax.rem(col + j + 1, cols_n)],
            lambda j: piece_recv.at[h, j],
            col_list,
        )
    totals = []
    for h in each:
        total = piece_send[h, col].astype(F32)
        for j, copy in enumerate(step[h]):
            copy.wait_recv()
            total = total + piece_recv[h, j].astype(F32)
        totals.append(total)
    total = jnp.transpose(jnp.concatenate(totals, 0))
    sub_out[1] = total[:piece]
    sub_out[2] = total[piece:]
    for copy in started:
        copy.wait_send()
    for stage in range(1, cols_n):
        for right in (True, False):
            copy, sends, unused = hop(right, stage)

            @pl.when(sends)
            def sent():
                copy.wait_send()


def fused(mesh):
    layers, rows_n, cols_n = (mesh.shape[a] for a in ("gz", "row", "col"))

    def local_fused(*args):
        anc_lower, anc_upper, sub_lower, sub_upper, anc_rhs, sub_rhs, subtree, pattern = args
        cut, right = anc_rhs.shape[1], anc_rhs.shape[2]
        anc_rhs = jnp.swapaxes(anc_rhs, 1, 2)
        sub_rhs = jnp.swapaxes(sub_rhs, 1, 2)
        pattern = jnp.swapaxes(pattern, 0, 1)
        args = args[:4] + (anc_rhs, sub_rhs, subtree, pattern)
        piece = cut // cols_n
        vec = (right // HALVES, cut)
        H = HALVES
        peers_n = max(rows_n, cols_n) - 1
        hbm = pl.BlockSpec(memory_space=pl.ANY)
        smem = pl.BlockSpec(memory_space=pltpu.SMEM)
        vmem = pl.BlockSpec(memory_space=pltpu.VMEM)
        return pl.pallas_call(
            functools.partial(fused_kernel, layers, rows_n, cols_n),
            out_shape=(
                pltpu.VMEM((1, piece, right), F32),
                pltpu.VMEM((SUB_NODES, piece, right), F32),
            ),
            in_specs=[hbm] * 6 + [smem] * 2,
            out_specs=(vmem, vmem),
            scratch_shapes=[
                pltpu.VMEM((rows_n, cut, cut), BF),
                pltpu.VMEM((cols_n, cut, cut // layers), BF),
                pltpu.VMEM(sub_lower.shape, BF),
                pltpu.VMEM(sub_upper.shape, BF),
                pltpu.VMEM(anc_rhs.shape, BF),
                pltpu.VMEM(sub_rhs.shape, BF),
                pltpu.VMEM((2, H, 2) + vec, BF),
                pltpu.VMEM((2, H, peers_n, 2) + vec, BF),
                pltpu.VMEM((7, H, 1) + vec, BF),
                pltpu.VMEM((7, H, peers_n, 1) + vec, BF),
                pltpu.VMEM((H, 1) + vec, BF),
                pltpu.VMEM((H, layers * rows_n - 1, 1) + vec, BF),
                pltpu.VMEM((1, cut, cut // layers), BF),
                pltpu.VMEM((layers, cut, cut // layers), BF),
                pltpu.VMEM((2, cut, right), F32),
                pltpu.VMEM((H, cols_n, right // H, 2 * piece), BF),
                pltpu.VMEM((H, cols_n - 1, right // H, 2 * piece), BF),
                pltpu.SemaphoreType.DMA((8,)),
                pltpu.SemaphoreType.DMA((H, 12, layers * rows_n)),
                pltpu.SemaphoreType.DMA((H, 12, layers * rows_n)),
            ],
            compiler_params=pltpu.CompilerParams(collective_id=0, has_side_effects=True),
        )(*args)

    return local_fused


def solution(mesh):
    in_specs = (
        P(None, "col", "row"),
        P(None, "col", "row"),
        P("gz", "col", "row"),
        P("gz", "col", "row"),
        P(None, "col", None),
        P("gz", "col", None),
        P(),
        P("gz", None),
    )
    out_specs = (P(None, ("row", "col"), None), P("gz", ("row", "col"), None))
    one_anc = mesh.shape["gz"] == 2
    square = mesh.shape["row"] == mesh.shape["col"] == 4
    body = fused(mesh) if one_anc and square else local
    return jax.shard_map(body, mesh=mesh, in_specs=in_specs, out_specs=out_specs, check_vma=False)
```
